32 devices in a mesh: row: 8 (over z, x), col: 4 (over y, core).
Axes of the slice: x: 2, y: 2, z: 4, core: 2. Of those that a mesh axis runs over, the one named last changes fastest.
Arguments:
- block_cost: bfloat16 [128, 16, 256, 256], P('row', 'col'), may hold values from 0 to 15, as said below
- candidates: int32 [128, 16], P('row', 'col'), may hold values from 0 to 31, all different within a row
- source_logmass: float32 [128, 256], P('row'), may hold values from -4 to 4
- target_logmass: float32 [32, 256], replicated, may hold values from -4 to 4
Outputs:
- source_potential: float32 [128, 256], P('row')
- target_potential: float32 [32, 256], replicated
The draws below stay inside these ranges and needn't reach their ends.
Inputs may be any that keep to these rules, and one draw needn't show every extreme that they name: Each row of candidates names 16 distinct target blocks, and every target block is named by some row. `block_cost`: costs are nonnegative.
All inputs are finite; a program needn't handle non-finite values.
Results may differ from the reference program's by a relative error of at most 0.0003.
Values sent between devices are 32-bit elements; how exact they have to be, the bound alone decides.
No kernel may reach another device: no remote copies, remote signals or barrier semaphores. Data moves between devices by JAX's collectives and lax.ppermute only.
A program may use at most 256 MiB of HBM per device.

```python
import jax
import jax.numpy as jnp
from jax import lax

BS = 256
K = 16
ITERS = 2
RB = 128
CB = 32


def draw_block_cost(key, part):
    first = jax.random.fold_in(key, 0)
    values = jax.random.uniform(first, (RB, K, BS, BS), jnp.float32, 0.0, 4.0)
    return values.astype(jnp.bfloat16)


def steps_of(stream_key, dims, pieces, low, high):
    loudness, own = 1.0, jax.random.fold_in(stream_key, 6)
    for dim, shards_of in pieces:
        steps = jnp.exp(jax.random.uniform(jax.random.fold_in(own, dim), (shards_of,), jnp.float32, low / len(pieces), high / len(pieces)))
        loudness = loudness * jnp.repeat(steps, dims[dim] // shards_of).reshape([-1 if axis == dim else 1 for axis in range(len(dims))])
    return loudness


def different_ones(rng, rows, count, top, lift):
    ranking = jax.random.permutation(jax.random.fold_in(rng, 1), count)
    boost = ranking
    for power in range(3):
        boost = boost * boost // count
    boost = boost * lift // count
    tickets = jax.random.randint(jax.random.fold_in(rng, 2), (rows, count), 0, 4096) + boost
    fixed_rows = jax.random.permutation(jax.random.fold_in(rng, 3), rows)[jnp.arange(count) % rows]
    tickets = jnp.where(jnp.arange(rows)[:, None] == fixed_rows[None, :], 1 << 14, tickets)
    merit = tickets * count + jnp.arange(count)
    return lax.top_k(merit.astype(jnp.int32), top)[1].astype(jnp.int32)


def setup_inputs(seed: int = 0) -> dict:
    key_of = jax.random.split(jax.random.key(seed), 5)
    return {
        "block_cost": draw_block_cost(jax.random.fold_in(key_of[4], 71), 0),
        "candidates": different_ones(key_of[1], RB, CB, K, 8192),
        "source_logmass": jnp.clip(jax.random.uniform(key_of[2], (RB, BS), jnp.float32, -4.0, 4.0) * steps_of(key_of[2], (RB, BS), ((0, 8),), -0.4, 0.0), -4.0, 4.0),
        "target_logmass": jnp.clip(jax.random.uniform(key_of[3], (CB, BS), jnp.float32, -4.0, 4.0), -4.0, 4.0),
    }


EPS = 0.05
LOWEST = -1.0e30


def reference(block_cost, candidates, source_logmass, target_logmass):
    target_pot = jnp.zeros((CB, BS), jnp.float32)
    source_pot = jnp.zeros((RB, BS), jnp.float32)
    flat_ids = candidates.reshape(-1).astype(jnp.int32)
    for step_index in range(ITERS):
        nearby = target_pot[candidates]

        def row_block(operands):
            costs, potential = operands
            scores = (potential[:, None, :] - costs.astype(jnp.float32)) / EPS
            highest = jnp.max(scores, axis=(0, 2))
            totals = jnp.sum(jnp.exp(scores - highest[None, :, None]), axis=(0, 2))
            return highest + jnp.log(totals)

        source_pot = EPS * source_logmass - EPS * lax.map(row_block, (block_cost, nearby))

        def col_block(operands):
            costs, potential = operands
            scores = (potential[None, :, None] - costs.astype(jnp.float32)) / EPS
            highest = jnp.max(scores, axis=1)
            totals = jnp.sum(jnp.exp(scores - highest[:, None, :]), axis=1)
            return highest, totals

        col_high, col_total = lax.map(col_block, (block_cost, source_pot))
        col_high = col_high.reshape(-1, BS)
        col_total = col_total.reshape(-1, BS)
        peaks = jnp.full((CB, BS), LOWEST, jnp.float32).at[flat_ids].max(col_high)
        masses = jnp.zeros((CB, BS), jnp.float32).at[flat_ids].add(col_total * jnp.exp(col_high - peaks[flat_ids]))
        target_pot = EPS * target_logmass - EPS * (peaks + jnp.log(masses))
    return source_pot, target_pot
```

```python
import functools
import math

import jax
import jax.numpy as jnp
from jax import lax
from jax.experimental import pallas as pl
from jax.experimental.pallas import tpu as pltpu
from jax.sharding import PartitionSpec as P

ITERS = 2
EPS = 0.05
LOWEST = -1e30
LOG2E = math.log2(math.e)
SCALE = LOG2E / EPS
LANES = 128
ROWS = 32


def log2(x):
    return jnp.log(x) * LOG2E


def add_exp2(a, b):
    high = jnp.maximum(a, b)
    return high + log2(1.0 + jnp.exp2(jnp.minimum(a, b) - high))


def bit_groups(size, sizes):
    bits = [1 << b for b in range(size.bit_length() - 1)]
    assert 1 << len(bits) == size
    groups = []
    while bits:
        take = sizes.pop(0) if sizes else 2
        groups.append(bits[:take])
        bits = bits[take:]
    return groups


def exchange(value, axes, size, bits):
    got = [value]
    offsets = [0]
    for bit in bits:
        offsets += [o | bit for o in offsets]
    for offset in offsets[1:]:
        got.append(lax.ppermute(value, axes, [(i, i ^ offset) for i in range(size)]))
    return got


def all_sum(value, axes, size, sizes):
    for bits in bit_groups(size, list(sizes)):
        value = functools.reduce(jnp.add, exchange(value, axes, size, bits))
    return value


def all_lse2(value, axes, size, sizes):
    for bits in bit_groups(size, list(sizes)):
        got = exchange(value, axes, size, bits)
        high = functools.reduce(jnp.maximum, got)
        value = high + log2(functools.reduce(jnp.add, [jnp.exp2(g - high) for g in got]))
    return value


def fetch(cost_hbm, cost, sems):
    def copy(r):
        return pltpu.make_async_copy(cost_hbm.at[r], cost.at[r], sems.at[r])

    for r in range(cost.shape[0]):
        copy(r).start()
    return copy


def lane_ids(rows):
    return lax.broadcasted_iota(jnp.int32, (rows, LANES), 1)


def lane_parts(width):
    return [pl.ds(start, LANES) for start in range(0, width, LANES)]


def put_column(acc, rows, column, r):
    acc[rows, :] = jnp.where(lane_ids(ROWS) == r, column, acc[rows, :])


def columns_of(source, flipped):
    count, points = source.shape
    full = jnp.concatenate([source[...], jnp.zeros((LANES - count, points), jnp.float32)], axis=0)
    flipped[...] = full.T


def column(flipped, rows, r):
    picked = jnp.where(lane_ids(ROWS) == r, flipped[rows, :], 0.0)
    return jnp.sum(picked, axis=1, keepdims=True)


def row_first_kernel(cost_hbm, out, cost, acc, sems):
    copy = fetch(cost_hbm, cost, sems)
    count, width, points, others = cost.shape

    def body(r, carry):
        copy(r).wait()
        for start in range(0, points, ROWS):
            rows = pl.ds(start, ROWS)
            blocks = [cost[r, k, rows, part] for k in range(width) for part in lane_parts(others)]
            low = functools.reduce(jnp.minimum, blocks).astype(jnp.float32)
            low = jnp.min(low, axis=1, keepdims=True)
            total = jnp.zeros((ROWS, LANES), jnp.float32)
            for block in blocks:
                total += jnp.exp2((low - block.astype(jnp.float32)) * SCALE)
            total = jnp.sum(total, axis=1, keepdims=True)
            put_column(acc, rows, log2(total) - low * SCALE, r)
        return carry

    lax.fori_loop(0, count, body, 0)
    out[...] = acc[...].T[:count]


def row_next_kernel(picks, cost_hbm, source, target, out, cost, acc, flipped, table, sems):
    copy = fetch(cost_hbm, cost, sems)
    columns_of(source, flipped)
    table[...] = target[...].reshape(table.shape)
    count, width, points, others = cost.shape

    def body(r, carry):
        copy(r).wait()
        aims = [table[picks[r, k], :, part] for k in range(width) for part in lane_parts(others)]
        for start in range(0, points, ROWS):
            rows = pl.ds(start, ROWS)
            mine = column(flipped, rows, r)
            total = jnp.zeros((ROWS, LANES), jnp.float32)
            spots = [(k, part) for k in range(width) for part in lane_parts(others)]
            for aim, (k, part) in zip(aims, spots):
                block = cost[r, k, rows, part].astype(jnp.float32)
                total += jnp.exp2((aim - block * SCALE) + mine)
            put_column(acc, rows, jnp.sum(total, axis=1, keepdims=True), r)
        return carry

    lax.fori_loop(0, count, body, 0)
    out[...] = acc[...].T[:count]


def col_first_kernel(picks, cost_hbm, source, out, cost, flipped, wide, near, table, sems):
    copy = fetch(cost_hbm, cost, sems)
    columns_of(source, flipped)
    table[...] = jnp.full(table.shape, LOWEST, jnp.float32)
    count, width, points, others = cost.shape

    def body(r, carry):
        for start in range(0, points, ROWS):
            rows = pl.ds(start, ROWS)
            spread = jnp.broadcast_to(column(flipped, rows, r), (ROWS, LANES))
            wide[rows, :] = spread
            near[rows, :] = (spread * (1.0 / SCALE)).astype(jnp.bfloat16)
        copy(r).wait()
        for k in range(width):
            for part in lane_parts(others):
                best = None
                for start in range(0, points, ROWS):
                    rows = pl.ds(start, ROWS)
                    gap = near[rows, :] - cost[r, k, rows, part]
                    best = gap if best is None else jnp.maximum(best, gap)
                peak = jnp.max(best.astype(jnp.float32), axis=0, keepdims=True) * SCALE
                total = jnp.zeros((ROWS, LANES), jnp.float32)
                for start in range(0, points, ROWS):
                    rows = pl.ds(start, ROWS)
                    block = cost[r, k, rows, part].astype(jnp.float32)
                    total += jnp.exp2((wide[rows, :] - block * SCALE) - peak)
                total = jnp.sum(total, axis=0, keepdims=True)
                spot = picks[r, k]
                table[spot, :, part] = add_exp2(table[spot, :, part], peak + log2(total))
        return carry

    lax.fori_loop(0, count, body, 0)
    out[...] = table[...].reshape(out.shape)


def col_next_kernel(picks, cost_hbm, source, target, out, cost, flipped, wide, table, sums, sems):
    copy = fetch(cost_hbm, cost, sems)
    columns_of(source, flipped)
    table[...] = target[...].reshape(table.shape)
    sums[...] = jnp.zeros(sums.shape, jnp.float32)
    count, width, points, others = cost.shape

    def body(r, carry):
        for start in range(0, points, ROWS):
            rows = pl.ds(start, ROWS)
            wide[rows, :] = jnp.broadcast_to(column(flipped, rows, r), (ROWS, LANES))
        copy(r).wait()
        for k in range(width):
            for part in lane_parts(others):
                spot = picks[r, k]
                aim = table[spot, :, part]
                total = jnp.zeros((ROWS, LANES), jnp.float32)
                for start in range(0, points, ROWS):
                    rows = pl.ds(start, ROWS)
                    block = cost[r, k, rows, part].astype(jnp.float32)
                    total += jnp.exp2((aim - block * SCALE) + wide[rows, :])
                sums[spot, :, part] += jnp.sum(total, axis=0, keepdims=True)
        return carry

    lax.fori_loop(0, count, body, 0)
    out[...] = sums[...].reshape(out.shape)


def call(kernel, out_rows, cost, picks, vectors, extra):
    count, width, points, others = cost.shape
    vmem = pl.BlockSpec(memory_space=pltpu.VMEM)
    specs = [pl.BlockSpec(memory_space=pl.ANY)] + [vmem] * len(vectors)
    args = [cost] + list(vectors)
    if picks is not None:
        specs = [pl.BlockSpec(memory_space=pltpu.SMEM)] + specs
        args = [picks] + args
    return pl.pallas_call(
        kernel,
        out_shape=jax.ShapeDtypeStruct((out_rows, points), jnp.float32),
        in_specs=specs,
        out_specs=vmem,
        scratch_shapes=[pltpu.VMEM(cost.shape, cost.dtype)]
        + extra
        + [pltpu.SemaphoreType.DMA((count,))],
        compiler_params=pltpu.CompilerParams(vmem_limit_bytes=24 << 20),
    )(*args)


def per_device(rows, cols, block_cost, candidates, source_logmass, target_logmass):
    count, _, points, _ = block_cost.shape
    targets = target_logmass.shape[0]
    assert count <= LANES and points % LANES == 0 and points % ROWS == 0
    tall = pltpu.VMEM((points, LANES), jnp.float32)
    tall16 = pltpu.VMEM((points, LANES), jnp.bfloat16)
    source_mass = source_logmass * LOG2E
    target_mass = target_logmass * LOG2E
    flat = pltpu.VMEM((targets, 1, points), jnp.float32)
    everyone = ("row", "col")
    n = rows * cols
    source = target = None
    for step_index in range(ITERS):
        if step_index == 0:
            scores = call(row_first_kernel, count, block_cost, None, [], [tall])
            source = source_mass - all_lse2(scores, "col", cols, (2,))
            scores = call(col_first_kernel, targets, block_cost, candidates, [source], [tall, tall, tall16, flat])
            target = target_mass - all_lse2(scores, everyone, n, (1, 2))
        else:
            sums = call(row_next_kernel, count, block_cost, candidates, [source, target], [tall, tall, flat])
            source = source + (source_mass - log2(all_sum(sums, "col", cols, (2,))))
            sums = call(col_next_kernel, targets, block_cost, candidates, [source, target], [tall, tall, flat, flat])
            target = target + (target_mass - log2(all_sum(sums, everyone, n, (1, 2))))
    return (source * (1.0 / SCALE), target * (1.0 / SCALE))


def solution(mesh):
    return jax.shard_map(
        functools.partial(per_device, mesh.shape["row"], mesh.shape["col"]),
        mesh=mesh,
        in_specs=(P("row", "col", None, None), P("row", "col"), P("row", None), P()),
        out_specs=(P("row", None), P()),
        check_vma=False,
    )
```

```python
import functools
import math

import jax
import jax.numpy as jnp
from jax import lax
from jax.experimental import pallas as pl
from jax.experimental.pallas import tpu as pltpu
from jax.sharding import PartitionSpec as P

ITERS = 2
EPS = 0.05
LOWEST = -1e30
LOG2E = math.log2(math.e)
SCALE = LOG2E / EPS
LANES = 128
TILE = 16


def log2(x):
    return jnp.log(x) * LOG2E


def add_exp2(a, b):
    high = jnp.maximum(a, b)
    return high + log2(1.0 + jnp.exp2(jnp.minimum(a, b) - high))


def bit_groups(size, sizes):
    bits = [1 << b for b in range(size.bit_length() - 1)]
    assert 1 << len(bits) == size
    groups = []
    while bits:
        take = sizes.pop(0) if sizes else 2
        groups.append(bits[:take])
        bits = bits[take:]
    return groups


def exchange(value, axes, size, bits):
    got = [value]
    offsets = [0]
    for bit in bits:
        offsets += [o | bit for o in offsets]
    for offset in offsets[1:]:
        got.append(lax.ppermute(value, axes, [(i, i ^ offset) for i in range(size)]))
    return got


def all_sum(value, axes, size, sizes):
    for bits in bit_groups(size, list(sizes)):
        value = functools.reduce(jnp.add, exchange(value, axes, size, bits))
    return value


def all_lse2(value, axes, size, sizes):
    for bits in bit_groups(size, list(sizes)):
        got = exchange(value, axes, size, bits)
        high = functools.reduce(jnp.maximum, got)
        value = high + log2(functools.reduce(jnp.add, [jnp.exp2(g - high) for g in got]))
    return value


def tiles_of(points):
    return [pl.ds(start, TILE) for start in range(0, points, TILE)]


def lane_ids():
    return lax.broadcasted_iota(jnp.int32, (TILE, LANES), 1)


def put_column(columns, rows, column, r):
    columns[rows, :] = jnp.where(lane_ids() == r, column, columns[rows, :])


def spread_column(columns, wide, r):
    for rows in tiles_of(wide.shape[0]):
        picked = jnp.where(lane_ids() == r, columns[rows, :], 0.0)
        wide[rows, :] = jnp.broadcast_to(jnp.sum(picked, axis=1, keepdims=True), (TILE, LANES))


def to_columns(source, columns):
    count, points = source.shape
    full = jnp.concatenate([source[...], jnp.zeros((LANES - count, points), jnp.float32)], axis=0)
    columns[...] = full.T


def place_of(picks, r, n, others):
    k, lane = divmod(n * LANES, others)
    return picks[k, r], slice(None), pl.ds(lane, LANES)


def row_first_kernel(cost_hbm, out, scaled, cost, sems, wide, lows, totals):
    count, width, points, others = cost.shape

    def copy(r):
        return pltpu.make_async_copy(cost_hbm.at[r], cost.at[r], sems.at[r])

    for r in range(count):
        copy(r).start()

    def body(r, carry):
        copy(r).wait()
        spots = [(k, pl.ds(lane, LANES)) for k in range(width) for lane in range(0, others, LANES)]
        for rows in tiles_of(points):
            low = functools.reduce(jnp.minimum, [cost[r, k, rows, part] for k, part in spots])
            low = jnp.min(low.astype(jnp.float32), axis=1, keepdims=True) * SCALE
            wide[rows, :] = jnp.broadcast_to(low, (TILE, LANES))
        for rows in tiles_of(points):
            low = wide[rows, :]
            total = jnp.zeros((TILE, LANES), jnp.float32)
            for n, (k, part) in enumerate(spots):
                value = cost[r, k, rows, part].astype(jnp.float32) * SCALE
                scaled[r, n, rows, :] = value
                total += jnp.exp2(low - value)
            put_column(lows, rows, low, r)
            put_column(totals, rows, jnp.sum(total, axis=1, keepdims=True), r)
        return carry

    lax.fori_loop(0, count, body, 0)
    out[...] = log2(totals[...].T[:count]) - lows[...].T[:count]


def col_first_kernel(others, picks, scaled, source, out, plan, peaks, wide, columns, table):
    to_columns(source, columns)
    table[...] = jnp.full(table.shape, LOWEST, jnp.float32)
    count, parts, points, _ = scaled.shape

    def body(r, carry):
        spread_column(columns, wide, r)
        for n in range(parts):
            peak = None
            for rows in tiles_of(points):
                value = (wide[rows, :] - scaled[r, n, rows, :]).astype(jnp.bfloat16)
                peak = value if peak is None else jnp.maximum(peak, value)
            peak = jnp.max(peak.astype(jnp.float32), axis=0, keepdims=True)
            total = jnp.zeros((TILE, LANES), jnp.float32)
            for rows in tiles_of(points):
                term = jnp.exp2((wide[rows, :] - scaled[r, n, rows, :]) - peak)
                plan[r, n, rows, :] = term
                total += term
            peaks[r, pl.ds(n, 1), :] = peak
            place = place_of(picks, r, n, others)
            total = jnp.sum(total, axis=0, keepdims=True)
            table[place] = add_exp2(table[place], peak + log2(total))
        return carry

    lax.fori_loop(0, count, body, 0)
    out[...] = table[...].reshape(out.shape)


def row_next_kernel(others, picks, plan, peaks, target, out, lifts, totals, table):
    table[...] = target[...].reshape(table.shape)
    count, parts, points, _ = plan.shape

    def body(r, carry):
        for n in range(parts):
            lifts[r, pl.ds(n, 1), :] = jnp.exp2(table[place_of(picks, r, n, others)] + peaks[r, pl.ds(n, 1), :])
        for rows in tiles_of(points):
            total = jnp.zeros((TILE, LANES), jnp.float32)
            for n in range(parts):
                total += plan[r, n, rows, :] * lifts[r, pl.ds(n, 1), :]
            put_column(totals, rows, jnp.sum(total, axis=1, keepdims=True), r)
        return carry

    lax.fori_loop(0, count, body, 0)
    out[...] = totals[...].T[:count]


def col_next_kernel(others, picks, plan, lifts, change, out, wide, columns, sums):
    to_columns(change, columns)
    sums[...] = jnp.zeros(sums.shape, jnp.float32)
    count, parts, points, _ = plan.shape

    def body(r, carry):
        spread_column(columns, wide, r)
        for n in range(parts):
            total = jnp.zeros((TILE, LANES), jnp.float32)
            for rows in tiles_of(points):
                total += plan[r, n, rows, :] * wide[rows, :]
            total = jnp.sum(total, axis=0, keepdims=True) * lifts[r, pl.ds(n, 1), :]
            sums[place_of(picks, r, n, others)] += total
        return carry

    lax.fori_loop(0, count, body, 0)
    out[...] = sums[...].reshape(out.shape)


VMEM = pl.BlockSpec(memory_space=pltpu.VMEM)
SMEM = pl.BlockSpec(memory_space=pltpu.SMEM)
HBM = pl.BlockSpec(memory_space=pltpu.HBM)


def call(kernel, outs, specs, scratch, megabytes, args):
    return pl.pallas_call(
        kernel,
        out_shape=outs,
        in_specs=specs,
        out_specs=[VMEM] * len(outs),
        scratch_shapes=scratch,
        compiler_params=pltpu.CompilerParams(vmem_limit_bytes=megabytes << 20),
    )(*args)


def per_device(rows, cols, block_cost, candidates, source_logmass, target_logmass):
    count, width, points, others = block_cost.shape
    targets = target_logmass.shape[0]
    parts = width * others // LANES
    assert count <= LANES and points % TILE == 0 and others % LANES == 0 and ITERS == 2
    f32 = jnp.float32
    by_source = jax.ShapeDtypeStruct((count, points), f32)
    by_target = jax.ShapeDtypeStruct((targets, others), f32)
    blocks = pltpu.VMEM((count, parts, points, LANES), f32)
    strips = pltpu.VMEM((count, parts, LANES), f32)
    tall = pltpu.VMEM((points, LANES), f32)
    flat = pltpu.VMEM((targets, 1, others), f32)
    source_mass = source_logmass * LOG2E
    target_mass = target_logmass * LOG2E
    picks = candidates.T
    everyone = ("row", "col")
    n = rows * cols

    landing = [pltpu.VMEM(block_cost.shape, block_cost.dtype), pltpu.SemaphoreType.DMA((count,))]
    scores, scaled = call(
        row_first_kernel, [by_source, blocks], [HBM], landing + [tall, tall, tall], 24, [pltpu.with_memory_space_constraint(block_cost, pltpu.HBM)]
    )
    source = source_mass - all_lse2(scores, "col", cols, (2,))
    scores, plan, peaks = call(
        functools.partial(col_first_kernel, others),
        [by_target, blocks, strips],
        [SMEM, VMEM, VMEM],
        [tall, tall, flat],
        8,
        [picks, scaled, source],
    )
    target = target_mass - all_lse2(scores, everyone, n, (1, 2))
    sums, lifts = call(
        functools.partial(row_next_kernel, others),
        [by_source, strips],
        [SMEM, VMEM, VMEM, VMEM],
        [tall, flat],
        8,
        [picks, plan, peaks, target],
    )
    change = source_mass - log2(all_sum(sums, "col", cols, (2,)))
    (sums,) = call(
        functools.partial(col_next_kernel, others),
        [by_target],
        [SMEM, VMEM, VMEM, VMEM],
        [tall, tall, flat],
        8,
        [picks, plan, lifts, jnp.exp2(change)],
    )
    target = target + (target_mass - log2(all_sum(sums, everyone, n, (1, 2))))
    return ((source + change) * (1.0 / SCALE), target * (1.0 / SCALE))


def solution(mesh):
    return jax.shard_map(
        functools.partial(per_device, mesh.shape["row"], mesh.shape["col"]),
        mesh=mesh,
        in_specs=(P("row", "col", None, None), P("row", "col"), P("row", None), P()),
        out_specs=(P("row", None), P()),
        check_vma=False,
    )
```

```python
import functools
import math

import jax
import jax.numpy as jnp
from jax import lax
from jax.experimental import pallas as pl
from jax.experimental.pallas import tpu as pltpu
from jax.sharding import PartitionSpec as P

ITERS = 2
EPS = 0.05
LOWEST = -1e30
LOG2E = math.log2(math.e)
SCALE = LOG2E / EPS
LANES = 128
TILE = 16
UNROLL = 4
GRANT = 14


def log2(x):
    return jnp.log(x) * LOG2E


def add_exp2(a, b):
    high = jnp.maximum(a, b)
    return high + log2(1.0 + jnp.exp2(jnp.minimum(a, b) - high))


def bit_groups(size, sizes):
    bits = [1 << b for b in range(size.bit_length() - 1)]
    assert 1 << len(bits) == size
    groups = []
    while bits:
        take = sizes.pop(0) if sizes else 2
        groups.append(bits[:take])
        bits = bits[take:]
    return groups


def exchange(value, axes, size, bits):
    got = [value]
    offsets = [0]
    for bit in bits:
        offsets += [o | bit for o in offsets]
    for offset in offsets[1:]:
        got.append(lax.ppermute(value, axes, [(i, i ^ offset) for i in range(size)]))
    return got


def all_sum(value, axes, size, sizes):
    for bits in bit_groups(size, list(sizes)):
        value = functools.reduce(jnp.add, exchange(value, axes, size, bits))
    return value


def all_lse2(value, axes, size, sizes):
    for bits in bit_groups(size, list(sizes)):
        got = exchange(value, axes, size, bits)
        high = functools.reduce(jnp.maximum, got)
        value = high + log2(functools.reduce(jnp.add, [jnp.exp2(g - high) for g in got]))
    return value


def tiles_of(points):
    return [pl.ds(start, TILE) for start in range(0, points, TILE)]


def lane_ids(rows, width=LANES):
    return lax.broadcasted_iota(jnp.int32, (rows, width), 1)


def put_column(columns, rows, column, r):
    columns[rows, :] = jnp.where(lane_ids(TILE) == r, column, columns[rows, :])


def spread_column(columns, wide, r):
    for rows in tiles_of(wide.shape[0]):
        picked = jnp.where(lane_ids(TILE) == r, columns[rows, :], 0.0)
        wide[rows, :] = jnp.broadcast_to(jnp.sum(picked, axis=1, keepdims=True), (TILE, LANES))


def to_columns(source, columns):
    count, points = source.shape
    full = jnp.concatenate([source, jnp.zeros((LANES - count, points), jnp.float32)], axis=0)
    columns[...] = full.T


def stacked(tables, height):
    rest = height - sum(table.shape[0] for table in tables)
    if rest:
        tables = tables + [jnp.zeros((rest, LANES), jnp.float32)]
    return jnp.concatenate(tables, axis=0)


def exact_dot(marked, table, dim):
    return lax.dot_general(
        marked,
        table,
        (((dim,), (0,)), ((), ())),
        precision=lax.Precision.HIGHEST,
        preferred_element_type=jnp.float32,
    )


def row_first_kernel(
    unroll, cost_hbm, source_hbm, target_hbm, scaled, out, source_mass, target_mass, cost, sems, wide, lows, totals
):
    count, width, points, others = cost.shape

    def copy(r):
        return pltpu.make_async_copy(cost_hbm.at[r], cost.at[r], sems.at[r])

    for r in range(count):
        copy(r).start()
    copies = [
        pltpu.make_async_copy(source_hbm, source_mass, sems.at[count]),
        pltpu.make_async_copy(target_hbm, target_mass, sems.at[count + 1]),
    ]
    for other in copies:
        other.start()

    def body(r, carry):
        copy(r).wait()
        spots = [(k, pl.ds(lane, LANES)) for k in range(width) for lane in range(0, others, LANES)]
        for rows in tiles_of(points):
            low = None
            for n, (k, part) in enumerate(spots):
                value = cost[r, k, rows, part].astype(jnp.float32) * SCALE
                scaled[r, n, rows, :] = value
                low = value if low is None else jnp.minimum(low, value)
            wide[rows, :] = jnp.broadcast_to(jnp.min(low, axis=1, keepdims=True), (TILE, LANES))
        for rows in tiles_of(points):
            low = wide[rows, :]
            total = jnp.zeros((TILE, LANES), jnp.float32)
            for n in range(len(spots)):
                total += jnp.exp2(low - scaled[r, n, rows, :])
            put_column(lows, rows, low, r)
            put_column(totals, rows, jnp.sum(total, axis=1, keepdims=True), r)
        return carry

    lax.fori_loop(0, count, body, 0, unroll=unroll)
    out[...] = log2(totals[...].T[:count]) - lows[...].T[:count]
    for other in copies:
        other.wait()


def col_first_kernel(
    unroll, picks_hbm, scaled, source, out, plan, peaks, marks, picks, sem, found, wide, columns
):
    copy = pltpu.make_async_copy(picks_hbm, picks, sem)
    copy.start()
    to_columns(source[...], columns)
    count, parts, points, _ = scaled.shape
    targets, others = out.shape
    split, height = others // LANES, marks.shape[2]

    def work(r):
        spread_column(columns, wide, r)
        for n in range(parts):
            peak = None
            for rows in tiles_of(points):
                value = wide[rows, :] - scaled[r, n, rows, :]
                peak = value if peak is None else jnp.maximum(peak, value)
            peak = jnp.max(peak, axis=0, keepdims=True)
            total = jnp.zeros((TILE, LANES), jnp.float32)
            for rows in tiles_of(points):
                term = jnp.exp2((wide[rows, :] - scaled[r, n, rows, :]) - peak)
                plan[r, n, rows, :] = term
                total += term
            peaks[r, pl.ds(n, 1), :] = peak
            found[r, pl.ds(n, 1), :] = peak + log2(jnp.sum(total, axis=0, keepdims=True))

    def work_step(r, carry):
        work(r)
        return carry

    lax.fori_loop(0, count, work_step, 0, unroll=unroll)
    copy.wait()

    own = lax.broadcasted_iota(jnp.int32, (targets, LANES), 0)

    def settle(r, best):
        best = list(best)
        for n in range(parts):
            k, h = divmod(n, split)
            mine = jnp.where(own == picks[k, r], found[r, pl.ds(n, 1), :], LOWEST)
            best[h] = jnp.maximum(best[h], mine)
            spot = h * targets + picks[k, r]
            marks[r, pl.ds(n, 1), :] = jnp.where(lane_ids(1, height) == spot, 1.0, 0.0)
        return tuple(best)

    lowest = jnp.full((targets, LANES), LOWEST, jnp.float32)
    best = lax.fori_loop(0, count, settle, (lowest,) * split, unroll=unroll)
    marked = marks[...].reshape(count * parts, height)
    mine = exact_dot(marked, stacked(list(best), height), 1)
    terms = jnp.exp2(found[...].reshape(count * parts, LANES) - mine)
    sums = exact_dot(marked, terms, 0)
    for h in range(split):
        total = sums[h * targets : (h + 1) * targets]
        named = total > 0.0
        score = jnp.where(named, best[h] + log2(jnp.where(named, total, 1.0)), LOWEST)
        out[:, h * LANES : (h + 1) * LANES] = score


def row_next_kernel(unroll, plan, peaks, marks, target, out, lifts, totals):
    count, parts, points, _ = plan.shape
    height = marks.shape[2]
    marked = marks[...].reshape(count * parts, height)
    tables = [target[:, lane : lane + LANES] for lane in range(0, target.shape[1], LANES)]
    mine = exact_dot(marked, stacked(tables, height), 1)
    lifts[...] = jnp.exp2(mine.reshape(lifts.shape) + peaks[...])

    def body(r, carry):
        for rows in tiles_of(points):
            total = jnp.zeros((TILE, LANES), jnp.float32)
            for n in range(parts):
                total += plan[r, n, rows, :] * lifts[r, pl.ds(n, 1), :]
            put_column(totals, rows, jnp.sum(total, axis=1, keepdims=True), r)
        return carry

    lax.fori_loop(0, count, body, 0, unroll=unroll)
    out[...] = totals[...].T[:count]


def col_next_kernel(
    unroll, plan, lifts, marks, source, change, out, source_hbm, result, sem, found, wide, columns
):
    count, parts, points, _ = plan.shape
    height = marks.shape[2]
    to_columns(jnp.exp2(change[...]), columns)
    result[...] = (source[...] + change[...]) * (1.0 / SCALE)
    copy = pltpu.make_async_copy(result, source_hbm, sem)
    copy.start()

    def body(r, carry):
        spread_column(columns, wide, r)
        for n in range(parts):
            total = jnp.zeros((TILE, LANES), jnp.float32)
            for rows in tiles_of(points):
                total += plan[r, n, rows, :] * wide[rows, :]
            found[r, pl.ds(n, 1), :] = jnp.sum(total, axis=0, keepdims=True) * lifts[r, pl.ds(n, 1), :]
        return carry

    lax.fori_loop(0, count, body, 0, unroll=unroll)
    sums = exact_dot(
        marks[...].reshape(count * parts, height), found[...].reshape(count * parts, LANES), 0
    )
    targets, others = out.shape
    for h in range(others // LANES):
        out[:, h * LANES : (h + 1) * LANES] = sums[h * targets : (h + 1) * targets]
    copy.wait()


VMEM = pl.BlockSpec(memory_space=pltpu.VMEM)
HBM = pl.BlockSpec(memory_space=pltpu.HBM)
COPY = pltpu.SemaphoreType.DMA


def call(name, kernel, outs, specs, scratch, megabytes, args):
    return pl.pallas_call(
        kernel,
        out_shape=outs,
        in_specs=specs,
        out_specs=[HBM if isinstance(out, jax.ShapeDtypeStruct) else VMEM for out in outs],
        scratch_shapes=scratch,
        compiler_params=pltpu.CompilerParams(vmem_limit_bytes=megabytes << 20),
        name=name,
    )(*args)


def in_hbm(value):
    return pltpu.with_memory_space_constraint(value, pltpu.HBM)


def per_device(rows, cols, block_cost, candidates, source_logmass, target_logmass):
    count, width, points, others = block_cost.shape
    targets = target_logmass.shape[0]
    parts = width * others // LANES
    assert count <= LANES and points % TILE == 0 and others % LANES == 0 and ITERS == 2
    height = -(-targets * (others // LANES) // LANES) * LANES
    f32 = jnp.float32
    by_source = pltpu.VMEM((count, points), f32)
    by_target = pltpu.VMEM((targets, others), f32)
    blocks = pltpu.VMEM((count, parts, points, LANES), f32)
    strips = pltpu.VMEM((count, parts, LANES), f32)
    marks = pltpu.VMEM((count, parts, height), f32)
    tall = pltpu.VMEM((points, LANES), f32)
    everyone = ("row", "col")
    n = rows * cols

    scaled, scores, source_mass, target_mass = call(
        "row_first",
        functools.partial(row_first_kernel, UNROLL),
        [blocks, by_source, by_source, by_target],
        [HBM, HBM, HBM],
        [pltpu.VMEM(block_cost.shape, block_cost.dtype), COPY((count + 2,)), tall, tall, tall],
        GRANT,
        [in_hbm(block_cost), in_hbm(source_logmass), in_hbm(target_logmass)],
    )
    source = source_mass * LOG2E - all_lse2(scores, "col", cols, (2,))
    picks = candidates.T
    scores, plan, peaks, marks = call(
        "col_first",
        functools.partial(col_first_kernel, UNROLL),
        [by_target, blocks, strips, marks],
        [HBM, VMEM, VMEM],
        [pltpu.SMEM(picks.shape, picks.dtype), COPY, strips, tall, tall],
        GRANT,
        [in_hbm(picks), scaled, source],
    )
    target = target_mass * LOG2E - all_lse2(scores, everyone, n, (1, 2))
    sums, lifts = call(
        "row_next",
        functools.partial(row_next_kernel, UNROLL),
        [by_source, strips],
        [VMEM] * 4,
        [tall],
        8,
        [plan, peaks, marks, target],
    )
    change = source_mass * LOG2E - log2(all_sum(sums, "col", cols, (2,)))
    sums, source = call(
        "col_next",
        functools.partial(col_next_kernel, UNROLL),
        [by_target, jax.ShapeDtypeStruct((count, points), f32)],
        [VMEM] * 5,
        [by_source, COPY, strips, tall, tall],
        8,
        [plan, lifts, marks, source, change],
    )
    target = target + (target_mass * LOG2E - log2(all_sum(sums, everyone, n, (1, 2))))
    return (source, target * (1.0 / SCALE))


def solution(mesh):
    return jax.shard_map(
        functools.partial(per_device, mesh.shape["row"], mesh.shape["col"]),
        mesh=mesh,
        in_specs=(P("row", "col", None, None), P("row", "col"), P("row", None), P()),
        out_specs=(P("row", None), P()),
        check_vma=False,
    )
```

```python
import functools
import math

import jax
import jax.numpy as jnp
from jax import lax
from jax.experimental import pallas as pl
from jax.experimental.pallas import tpu as pltpu
from jax.sharding import PartitionSpec as P

ITERS = 2
EPS = 0.05
LOWEST = -1e30
LOG2E = math.log2(math.e)
SCALE = LOG2E / EPS
LANES = 128
TILE = 16
UNROLL = 8
GRANT = 14


def log2(x):
    return jnp.log(x) * LOG2E


def add_exp2(a, b):
    high = jnp.maximum(a, b)
    return high + log2(1.0 + jnp.exp2(jnp.minimum(a, b) - high))


def bit_groups(size, sizes):
    bits = [1 << b for b in range(size.bit_length() - 1)]
    assert 1 << len(bits) == size
    groups = []
    while bits:
        take = sizes.pop(0) if sizes else 2
        groups.append(bits[:take])
        bits = bits[take:]
    return groups


def exchange(value, axes, size, bits):
    got = [value]
    offsets = [0]
    for bit in bits:
        offsets += [o | bit for o in offsets]
    for offset in offsets[1:]:
        got.append(lax.ppermute(value, axes, [(i, i ^ offset) for i in range(size)]))
    return got


def all_sum(value, axes, size, sizes):
    for bits in bit_groups(size, list(sizes)):
        value = functools.reduce(jnp.add, exchange(value, axes, size, bits))
    return value


def all_lse2(value, axes, size, sizes):
    for bits in bit_groups(size, list(sizes)):
        got = exchange(value, axes, size, bits)
        high = functools.reduce(jnp.maximum, got)
        value = high + log2(functools.reduce(jnp.add, [jnp.exp2(g - high) for g in got]))
    return value


def tiles_of(points):
    return [pl.ds(start, TILE) for start in range(0, points, TILE)]


def lane_ids(rows, width=LANES):
    return lax.broadcasted_iota(jnp.int32, (rows, width), 1)


def put_column(columns, rows, column, r):
    columns[rows, :] = jnp.where(lane_ids(TILE) == r, column, columns[rows, :])


def spread_column(columns, wide, r):
    for rows in tiles_of(wide.shape[0]):
        picked = jnp.where(lane_ids(TILE) == r, columns[rows, :], 0.0)
        wide[rows, :] = jnp.broadcast_to(jnp.sum(picked, axis=1, keepdims=True), (TILE, LANES))


def to_columns(source, columns):
    count, points = source.shape
    full = jnp.concatenate([source, jnp.zeros((LANES - count, points), jnp.float32)], axis=0)
    columns[...] = full.T


def stacked(tables, height):
    rest = height - sum(table.shape[0] for table in tables)
    if rest:
        tables = tables + [jnp.zeros((rest, LANES), jnp.float32)]
    return jnp.concatenate(tables, axis=0)


def exact_dot(marked, table, dim):
    return lax.dot_general(
        marked,
        table,
        (((dim,), (0,)), ((), ())),
        precision=lax.Precision.HIGHEST,
        preferred_element_type=jnp.float32,
    )


def row_first_kernel(
    unroll, cost_hbm, source_hbm, target_hbm, scaled, out, source_mass, target_mass, cost, sems, wide, lows, totals
):
    count, width, points, others = cost.shape

    def copy(r):
        return pltpu.make_async_copy(cost_hbm.at[r], cost.at[r], sems.at[r])

    for r in range(count):
        copy(r).start()
    copies = [
        pltpu.make_async_copy(source_hbm, source_mass, sems.at[count]),
        pltpu.make_async_copy(target_hbm, target_mass, sems.at[count + 1]),
    ]
    for other in copies:
        other.start()

    def body(r, carry):
        copy(r).wait()
        spots = [(k, pl.ds(lane, LANES)) for k in range(width) for lane in range(0, others, LANES)]
        for rows in tiles_of(points):
            low = None
            for n, (k, part) in enumerate(spots):
                value = cost[r, k, rows, part].astype(jnp.float32)
                scaled[r, n, rows, :] = value
                low = value if low is None else jnp.minimum(low, value)
            low = jnp.min(low, axis=1, keepdims=True) * SCALE
            wide[rows, :] = jnp.broadcast_to(low, (TILE, LANES))
        for rows in tiles_of(points):
            low = wide[rows, :]
            total = jnp.zeros((TILE, LANES), jnp.float32)
            for n in range(len(spots)):
                value = scaled[r, n, rows, :] * SCALE
                scaled[r, n, rows, :] = value
                total += jnp.exp2(low - value)
            put_column(lows, rows, low, r)
            put_column(totals, rows, jnp.sum(total, axis=1, keepdims=True), r)
        return carry

    lax.fori_loop(0, count, body, 0, unroll=unroll)
    out[...] = log2(totals[...].T[:count]) - lows[...].T[:count]
    for other in copies:
        other.wait()


def col_first_kernel(
    unroll, picks_hbm, scaled, source, out, plan, peaks, marks, picks, sem, found, wide, columns
):
    copy = pltpu.make_async_copy(picks_hbm, picks, sem)
    copy.start()
    to_columns(source[...], columns)
    count, parts, points, _ = scaled.shape
    targets, others = out.shape
    split, height = others // LANES, marks.shape[2]

    def work(r):
        spread_column(columns, wide, r)
        for n in range(parts):
            peak = None
            for rows in tiles_of(points):
                value = wide[rows, :] - scaled[r, n, rows, :]
                peak = value if peak is None else jnp.maximum(peak, value)
            peak = jnp.max(peak, axis=0, keepdims=True)
            total = jnp.zeros((TILE, LANES), jnp.float32)
            for rows in tiles_of(points):
                term = jnp.exp2((wide[rows, :] - scaled[r, n, rows, :]) - peak)
                plan[r, n, rows, :] = term
                total += term
            peaks[r, pl.ds(n, 1), :] = peak
            found[r, pl.ds(n, 1), :] = peak + log2(jnp.sum(total, axis=0, keepdims=True))

    def work_step(r, carry):
        work(r)
        return carry

    lax.fori_loop(0, count, work_step, 0, unroll=unroll)
    copy.wait()

    own = lax.broadcasted_iota(jnp.int32, (targets, LANES), 0)

    def settle(r, best):
        best = list(best)
        for n in range(parts):
            k, h = divmod(n, split)
            mine = jnp.where(own == picks[k, r], found[r, pl.ds(n, 1), :], LOWEST)
            best[h] = jnp.maximum(best[h], mine)
            spot = h * targets + picks[k, r]
            marks[r, pl.ds(n, 1), :] = jnp.where(lane_ids(1, height) == spot, 1.0, 0.0)
        return tuple(best)

    lowest = jnp.full((targets, LANES), LOWEST, jnp.float32)
    best = lax.fori_loop(0, count, settle, (lowest,) * split, unroll=unroll)
    marked = marks[...].reshape(count * parts, height)
    mine = exact_dot(marked, stacked(list(best), height), 1)
    terms = jnp.exp2(found[...].reshape(count * parts, LANES) - mine)
    sums = exact_dot(marked, terms, 0)
    for h in range(split):
        total = sums[h * targets : (h + 1) * targets]
        named = total > 0.0
        score = jnp.where(named, best[h] + log2(jnp.where(named, total, 1.0)), LOWEST)
        out[:, h * LANES : (h + 1) * LANES] = score


def row_next_kernel(unroll, plan, peaks, marks, target, out, lifts, totals):
    count, parts, points, _ = plan.shape
    height = marks.shape[2]
    marked = marks[...].reshape(count * parts, height)
    tables = [target[:, lane : lane + LANES] for lane in range(0, target.shape[1], LANES)]
    mine = exact_dot(marked, stacked(tables, height), 1)
    lifts[...] = jnp.exp2(mine.reshape(lifts.shape) + peaks[...])

    def body(r, carry):
        for rows in tiles_of(points):
            total = jnp.zeros((TILE, LANES), jnp.float32)
            for n in range(parts):
                total += plan[r, n, rows, :] * lifts[r, pl.ds(n, 1), :]
            put_column(totals, rows, jnp.sum(total, axis=1, keepdims=True), r)
        return carry

    lax.fori_loop(0, count, body, 0, unroll=unroll)
    out[...] = totals[...].T[:count]


def col_next_kernel(
    unroll, plan, lifts, marks, source, change, out, source_hbm, result, sem, found, wide, columns
):
    count, parts, points, _ = plan.shape
    height = marks.shape[2]
    to_columns(jnp.exp2(change[...]), columns)
    result[...] = (source[...] + change[...]) * (1.0 / SCALE)
    copy = pltpu.make_async_copy(result, source_hbm, sem)
    copy.start()

    def body(r, carry):
        spread_column(columns, wide, r)
        for n in range(parts):
            total = jnp.zeros((TILE, LANES), jnp.float32)
            for rows in tiles_of(points):
                total += plan[r, n, rows, :] * wide[rows, :]
            found[r, pl.ds(n, 1), :] = jnp.sum(total, axis=0, keepdims=True) * lifts[r, pl.ds(n, 1), :]
        return carry

    lax.fori_loop(0, count, body, 0, unroll=unroll)
    sums = exact_dot(
        marks[...].reshape(count * parts, height), found[...].reshape(count * parts, LANES), 0
    )
    targets, others = out.shape
    for h in range(others // LANES):
        out[:, h * LANES : (h + 1) * LANES] = sums[h * targets : (h + 1) * targets]
    copy.wait()


VMEM = pl.BlockSpec(memory_space=pltpu.VMEM)
HBM = pl.BlockSpec(memory_space=pltpu.HBM)
COPY = pltpu.SemaphoreType.DMA


def call(name, kernel, outs, specs, scratch, megabytes, args):
    return pl.pallas_call(
        kernel,
        out_shape=outs,
        in_specs=specs,
        out_specs=[HBM if isinstance(out, jax.ShapeDtypeStruct) else VMEM for out in outs],
        scratch_shapes=scratch,
        compiler_params=pltpu.CompilerParams(vmem_limit_bytes=megabytes << 20),
        name=name,
    )(*args)


def in_hbm(value):
    return pltpu.with_memory_space_constraint(value, pltpu.HBM)


def per_device(rows, cols, block_cost, candidates, source_logmass, target_logmass):
    count, width, points, others = block_cost.shape
    targets = target_logmass.shape[0]
    parts = width * others // LANES
    assert count <= LANES and points % TILE == 0 and others % LANES == 0 and ITERS == 2
    height = -(-targets * (others // LANES) // LANES) * LANES
    f32 = jnp.float32
    by_source = pltpu.VMEM((count, points), f32)
    by_target = pltpu.VMEM((targets, others), f32)
    blocks = pltpu.VMEM((count, parts, points, LANES), f32)
    strips = pltpu.VMEM((count, parts, LANES), f32)
    marks = pltpu.VMEM((count, parts, height), f32)
    tall = pltpu.VMEM((points, LANES), f32)
    everyone = ("row", "col")
    n = rows * cols

    scaled, scores, source_mass, target_mass = call(
        "row_first",
        functools.partial(row_first_kernel, UNROLL),
        [blocks, by_source, by_source, by_target],
        [HBM, HBM, HBM],
        [pltpu.VMEM(block_cost.shape, block_cost.dtype), COPY((count + 2,)), tall, tall, tall],
        GRANT,
        [in_hbm(block_cost), in_hbm(source_logmass), in_hbm(target_logmass)],
    )
    source = source_mass * LOG2E - all_lse2(scores, "col", cols, (2,))
    picks = candidates.T
    scores, plan, peaks, marks = call(
        "col_first",
        functools.partial(col_first_kernel, UNROLL),
        [by_target, blocks, strips, marks],
        [HBM, VMEM, VMEM],
        [pltpu.SMEM(picks.shape, picks.dtype), COPY, strips, tall, tall],
        GRANT,
        [in_hbm(picks), scaled, source],
    )
    target = target_mass * LOG2E - all_lse2(scores, everyone, n, (1, 2))
    sums, lifts = call(
        "row_next",
        functools.partial(row_next_kernel, UNROLL),
        [by_source, strips],
        [VMEM] * 4,
        [tall],
        8,
        [plan, peaks, marks, target],
    )
    change = source_mass * LOG2E - log2(all_sum(sums, "col", cols, (2,)))
    sums, source = call(
        "col_next",
        functools.partial(col_next_kernel, UNROLL),
        [by_target, jax.ShapeDtypeStruct((count, points), f32)],
        [VMEM] * 5,
        [by_source, COPY, strips, tall, tall],
        8,
        [plan, lifts, marks, source, change],
    )
    target = target + (target_mass * LOG2E - log2(all_sum(sums, everyone, n, (1, 2))))
    return (source, target * (1.0 / SCALE))


def solution(mesh):
    return jax.shard_map(
        functools.partial(per_device, mesh.shape["row"], mesh.shape["col"]),
        mesh=mesh,
        in_specs=(P("row", "col", None, None), P("row", "col"), P("row", None), P()),
        out_specs=(P("row", None), P()),
        check_vma=False,
    )
```

```python
import functools
import math

import jax
import jax.numpy as jnp
from jax import lax
from jax.experimental import pallas as pl
from jax.experimental.pallas import tpu as pltpu
from jax.sharding import PartitionSpec as P

ITERS = 2
EPS = 0.05
LOWEST = -1e30
SMALLEST = 2.0**-20
LOG2E = math.log2(math.e)
SCALE = LOG2E / EPS
LANES = 128
TILE = 16
UNROLL = 8
GRANT = 14


def log2(x):
    return jnp.log(x) * LOG2E


def add_exp2(a, b):
    high = jnp.maximum(a, b)
    return high + log2(1.0 + jnp.exp2(jnp.minimum(a, b) - high))


def bit_groups(size, sizes):
    bits = [1 << b for b in range(size.bit_length() - 1)]
    assert 1 << len(bits) == size
    groups = []
    while bits:
        take = sizes.pop(0) if sizes else 2
        groups.append(bits[:take])
        bits = bits[take:]
    return groups


def exchange(value, axes, size, bits):
    got = [value]
    offsets = [0]
    for bit in bits:
        offsets += [o | bit for o in offsets]
    for offset in offsets[1:]:
        got.append(lax.ppermute(value, axes, [(i, i ^ offset) for i in range(size)]))
    return got


def all_sum(value, axes, size, sizes):
    for bits in bit_groups(size, list(sizes)):
        value = functools.reduce(jnp.add, exchange(value, axes, size, bits))
    return value


def all_lse2(value, axes, size, sizes):
    for bits in bit_groups(size, list(sizes)):
        got = exchange(value, axes, size, bits)
        high = functools.reduce(jnp.maximum, got)
        value = high + log2(functools.reduce(jnp.add, [jnp.exp2(g - high) for g in got]))
    return value


def tiles_of(points):
    return [pl.ds(start, TILE) for start in range(0, points, TILE)]


def lane_ids(rows, width=LANES):
    return lax.broadcasted_iota(jnp.int32, (rows, width), 1)


def put_column(columns, rows, column, r):
    columns[rows, :] = jnp.where(lane_ids(TILE) == r, column, columns[rows, :])


def spread_column(columns, wide, r):
    for rows in tiles_of(wide.shape[0]):
        picked = jnp.where(lane_ids(TILE) == r, columns[rows, :], 0.0)
        wide[rows, :] = jnp.broadcast_to(jnp.sum(picked, axis=1, keepdims=True), (TILE, LANES))


def to_columns(source, columns):
    count, points = source.shape
    full = jnp.concatenate([source, jnp.zeros((LANES - count, points), jnp.float32)], axis=0)
    columns[...] = full.T


def stacked(tables, height):
    rest = height - sum(table.shape[0] for table in tables)
    if rest:
        tables = tables + [jnp.zeros((rest, LANES), jnp.float32)]
    return jnp.concatenate(tables, axis=0)


def exact_dot(marked, table, dim):
    return lax.dot_general(
        marked,
        table,
        (((dim,), (0,)), ((), ())),
        precision=lax.Precision.HIGHEST,
        preferred_element_type=jnp.float32,
    )


def row_first_kernel(
    unroll, cost_hbm, source_hbm, target_hbm, plan, out, lows_out, source_mass, target_mass, cost, sems, wide, lows, totals
):
    count, width, points, others = cost.shape

    def copy(r):
        return pltpu.make_async_copy(cost_hbm.at[r], cost.at[r], sems.at[r])

    for r in range(count):
        copy(r).start()
    copies = [
        pltpu.make_async_copy(source_hbm, source_mass, sems.at[count]),
        pltpu.make_async_copy(target_hbm, target_mass, sems.at[count + 1]),
    ]
    for other in copies:
        other.start()

    def body(r, carry):
        copy(r).wait()
        spots = [(k, pl.ds(lane, LANES)) for k in range(width) for lane in range(0, others, LANES)]
        for rows in tiles_of(points):
            low = None
            for n, (k, part) in enumerate(spots):
                value = cost[r, k, rows, part].astype(jnp.float32) * SCALE
                plan[r, n, rows, :] = value
                low = value if low is None else jnp.minimum(low, value)
            wide[rows, :] = jnp.broadcast_to(jnp.min(low, axis=1, keepdims=True), (TILE, LANES))
        for rows in tiles_of(points):
            low = wide[rows, :]
            total = jnp.zeros((TILE, LANES), jnp.float32)
            for n in range(len(spots)):
                term = jnp.exp2(low - plan[r, n, rows, :])
                plan[r, n, rows, :] = term
                total += term
            put_column(lows, rows, low, r)
            put_column(totals, rows, jnp.sum(total, axis=1, keepdims=True), r)
        return carry

    lax.fori_loop(0, count, body, 0, unroll=unroll)
    lows_out[...] = lows[...].T[:count]
    out[...] = log2(totals[...].T[:count]) - lows_out[...]
    for other in copies:
        other.wait()


def col_first_kernel(
    unroll, picks_hbm, cost_hbm, plan_in, source, lows, out, plan, peaks, marks, base, picks, sems, cost, found, wide, columns
):
    copy = pltpu.make_async_copy(picks_hbm, picks, sems.at[0])
    copy.start()
    base[...] = source[...] - lows[...]
    peaks[...] = jnp.zeros(peaks.shape, jnp.float32)
    to_columns(jnp.exp2(base[...]), columns)
    count, parts, points, _ = plan.shape
    targets, others = out.shape
    split, height = others // LANES, marks.shape[2]
    tiles = tiles_of(points)

    def work(r, carry):
        spread_column(columns, wide, r)
        for n in range(parts):
            total = jnp.zeros((TILE, LANES), jnp.float32)
            for rows in tiles:
                total += plan_in[r, n, rows, :] * wide[rows, :]
            found[r, pl.ds(n, 1), :] = jnp.sum(total, axis=0, keepdims=True)
        return carry

    lax.fori_loop(0, count, work, 0, unroll=unroll)

    @pl.when(jnp.logical_not(jnp.min(found[...]) >= SMALLEST))
    def _():
        to_columns(source[...], columns)
        base[...] = jnp.zeros(base.shape, jnp.float32)

        def again(r, carry):
            block = pltpu.make_async_copy(cost_hbm.at[r], cost, sems.at[1])
            block.start()
            spread_column(columns, wide, r)
            block.wait()
            for n in range(parts):
                k, h = divmod(n, split)
                part = pl.ds(h * LANES, LANES)
                peak = None
                for rows in tiles:
                    value = wide[rows, :] - cost[k, rows, part].astype(jnp.float32) * SCALE
                    peak = value if peak is None else jnp.maximum(peak, value)
                peak = jnp.max(peak, axis=0, keepdims=True)
                total = jnp.zeros((TILE, LANES), jnp.float32)
                for rows in tiles:
                    value = wide[rows, :] - cost[k, rows, part].astype(jnp.float32) * SCALE
                    term = jnp.exp2(value - peak)
                    plan[r, n, rows, :] = term
                    total += term
                peaks[r, pl.ds(n, 1), :] = peak
                found[r, pl.ds(n, 1), :] = jnp.sum(total, axis=0, keepdims=True)
            return carry

        lax.fori_loop(0, count, again, 0)

    found[...] = peaks[...] + log2(found[...])
    copy.wait()

    own = lax.broadcasted_iota(jnp.int32, (targets, LANES), 0)

    def settle(r, best):
        best = list(best)
        for n in range(parts):
            k, h = divmod(n, split)
            mine = jnp.where(own == picks[k, r], found[r, pl.ds(n, 1), :], LOWEST)
            best[h] = jnp.maximum(best[h], mine)
            spot = h * targets + picks[k, r]
            marks[r, pl.ds(n, 1), :] = jnp.where(lane_ids(1, height) == spot, 1.0, 0.0)
        return tuple(best)

    lowest = jnp.full((targets, LANES), LOWEST, jnp.float32)
    best = lax.fori_loop(0, count, settle, (lowest,) * split, unroll=unroll)
    marked = marks[...].reshape(count * parts, height)
    mine = exact_dot(marked, stacked(list(best), height), 1)
    terms = jnp.exp2(found[...].reshape(count * parts, LANES) - mine)
    sums = exact_dot(marked, terms, 0)
    for h in range(split):
        total = sums[h * targets : (h + 1) * targets]
        named = total > 0.0
        score = jnp.where(named, best[h] + log2(jnp.where(named, total, 1.0)), LOWEST)
        out[:, h * LANES : (h + 1) * LANES] = score


def row_next_kernel(unroll, plan, peaks, marks, target, base, out, lifts, totals):
    count, parts, points, _ = plan.shape
    height = marks.shape[2]
    marked = marks[...].reshape(count * parts, height)
    tables = [target[:, lane : lane + LANES] for lane in range(0, target.shape[1], LANES)]
    mine = exact_dot(marked, stacked(tables, height), 1)
    lifts[...] = jnp.exp2(mine.reshape(lifts.shape) + peaks[...])

    def body(r, carry):
        for rows in tiles_of(points):
            total = jnp.zeros((TILE, LANES), jnp.float32)
            for n in range(parts):
                total += plan[r, n, rows, :] * lifts[r, pl.ds(n, 1), :]
            put_column(totals, rows, jnp.sum(total, axis=1, keepdims=True), r)
        return carry

    lax.fori_loop(0, count, body, 0, unroll=unroll)
    out[...] = totals[...].T[:count] * jnp.exp2(base[...])


def col_next_kernel(
    unroll, plan, lifts, marks, source, change, base, out, source_hbm, result, sem, found, wide, columns
):
    count, parts, points, _ = plan.shape
    height = marks.shape[2]
    to_columns(jnp.exp2(change[...] + base[...]), columns)
    result[...] = (source[...] + change[...]) * (1.0 / SCALE)
    copy = pltpu.make_async_copy(result, source_hbm, sem)
    copy.start()

    def body(r, carry):
        spread_column(columns, wide, r)
        for n in range(parts):
            total = jnp.zeros((TILE, LANES), jnp.float32)
            for rows in tiles_of(points):
                total += plan[r, n, rows, :] * wide[rows, :]
            found[r, pl.ds(n, 1), :] = jnp.sum(total, axis=0, keepdims=True) * lifts[r, pl.ds(n, 1), :]
        return carry

    lax.fori_loop(0, count, body, 0, unroll=unroll)
    sums = exact_dot(
        marks[...].reshape(count * parts, height), found[...].reshape(count * parts, LANES), 0
    )
    targets, others = out.shape
    for h in range(others // LANES):
        out[:, h * LANES : (h + 1) * LANES] = sums[h * targets : (h + 1) * targets]
    copy.wait()


VMEM = pl.BlockSpec(memory_space=pltpu.VMEM)
HBM = pl.BlockSpec(memory_space=pltpu.HBM)
COPY = pltpu.SemaphoreType.DMA


def call(name, kernel, outs, specs, scratch, megabytes, args, aliases=()):
    return pl.pallas_call(
        kernel,
        out_shape=outs,
        in_specs=specs,
        out_specs=[HBM if isinstance(out, jax.ShapeDtypeStruct) else VMEM for out in outs],
        scratch_shapes=scratch,
        compiler_params=pltpu.CompilerParams(vmem_limit_bytes=megabytes << 20),
        name=name,
        input_output_aliases=dict(aliases),
    )(*args)


def in_hbm(value):
    return pltpu.with_memory_space_constraint(value, pltpu.HBM)


def per_device(rows, cols, block_cost, candidates, source_logmass, target_logmass):
    count, width, points, others = block_cost.shape
    targets = target_logmass.shape[0]
    parts = width * others // LANES
    assert count <= LANES and points % TILE == 0 and others % LANES == 0 and ITERS == 2
    height = -(-targets * (others // LANES) // LANES) * LANES
    f32 = jnp.float32
    by_source = pltpu.VMEM((count, points), f32)
    by_target = pltpu.VMEM((targets, others), f32)
    blocks = pltpu.VMEM((count, parts, points, LANES), f32)
    strips = pltpu.VMEM((count, parts, LANES), f32)
    marks = pltpu.VMEM((count, parts, height), f32)
    tall = pltpu.VMEM((points, LANES), f32)
    everyone = ("row", "col")
    n = rows * cols

    plan, scores, lows, source_mass, target_mass = call(
        "row_first",
        functools.partial(row_first_kernel, UNROLL),
        [blocks, by_source, by_source, by_source, by_target],
        [HBM, HBM, HBM],
        [pltpu.VMEM(block_cost.shape, block_cost.dtype), COPY((count + 2,)), tall, tall, tall],
        GRANT,
        [in_hbm(block_cost), in_hbm(source_logmass), in_hbm(target_logmass)],
    )
    source = source_mass * LOG2E - all_lse2(scores, "col", cols, (2,))
    picks = candidates.T
    scores, plan, peaks, marks, base = call(
        "col_first",
        functools.partial(col_first_kernel, UNROLL),
        [by_target, blocks, strips, marks, by_source],
        [HBM, HBM, VMEM, VMEM, VMEM],
        [pltpu.SMEM(picks.shape, picks.dtype), COPY((2,)), pltpu.VMEM(block_cost.shape[1:], block_cost.dtype)]
        + [strips, tall, tall],
        GRANT,
        [in_hbm(picks), in_hbm(block_cost), plan, source, lows],
        [(2, 1)],
    )
    target = target_mass * LOG2E - all_lse2(scores, everyone, n, (1, 2))
    sums, lifts = call(
        "row_next",
        functools.partial(row_next_kernel, UNROLL),
        [by_source, strips],
        [VMEM] * 5,
        [tall],
        8,
        [plan, peaks, marks, target, base],
    )
    change = source_mass * LOG2E - log2(all_sum(sums, "col", cols, (2,)))
    sums, source = call(
        "col_next",
        functools.partial(col_next_kernel, UNROLL),
        [by_target, jax.ShapeDtypeStruct((count, points), f32)],
        [VMEM] * 6,
        [by_source, COPY, strips, tall, tall],
        8,
        [plan, lifts, marks, source, change, base],
    )
    target = target + (target_mass * LOG2E - log2(all_sum(sums, everyone, n, (1, 2))))
    return (source, target * (1.0 / SCALE))


def solution(mesh):
    return jax.shard_map(
        functools.partial(per_device, mesh.shape["row"], mesh.shape["col"]),
        mesh=mesh,
        in_specs=(P("row", "col", None, None), P("row", "col"), P("row", None), P()),
        out_specs=(P("row", None), P()),
        check_vma=False,
    )
```

```python
import functools
import math

import jax
import jax.numpy as jnp
from jax import lax
from jax.experimental import pallas as pl
from jax.experimental.pallas import tpu as pltpu
from jax.sharding import PartitionSpec as P

ITERS = 2
EPS = 0.05
LOWEST = -1e30
SMALLEST = 2.0**-20
LOG2E = math.log2(math.e)
SCALE = LOG2E / EPS
LANES = 128
TILE = 16
UNROLL = 8
GRANT = 14


def log2(x):
    return jnp.log(x) * LOG2E


def add_exp2(a, b):
    high = jnp.maximum(a, b)
    return high + log2(1.0 + jnp.exp2(jnp.minimum(a, b) - high))


def bit_groups(size, sizes):
    bits = [1 << b for b in range(size.bit_length() - 1)]
    assert 1 << len(bits) == size
    groups = []
    while bits:
        take = sizes.pop(0) if sizes else 2
        groups.append(bits[:take])
        bits = bits[take:]
    return groups


def exchange(value, axes, size, bits):
    got = [value]
    offsets = [0]
    for bit in bits:
        offsets += [o | bit for o in offsets]
    for offset in offsets[1:]:
        got.append(lax.ppermute(value, axes, [(i, i ^ offset) for i in range(size)]))
    return got


def all_sum(value, axes, size, sizes):
    for bits in bit_groups(size, list(sizes)):
        value = functools.reduce(jnp.add, exchange(value, axes, size, bits))
    return value


def all_lse2(value, axes, size, sizes):
    for bits in bit_groups(size, list(sizes)):
        got = exchange(value, axes, size, bits)
        high = functools.reduce(jnp.maximum, got)
        value = high + log2(functools.reduce(jnp.add, [jnp.exp2(g - high) for g in got]))
    return value


def tiles_of(points):
    return [pl.ds(start, TILE) for start in range(0, points, TILE)]


def lane_ids(rows, width=LANES):
    return lax.broadcasted_iota(jnp.int32, (rows, width), 1)


def put_column(columns, rows, column, r):
    columns[rows, :] = jnp.where(lane_ids(TILE) == r, column, columns[rows, :])


def spread_column(columns, wide, r):
    for rows in tiles_of(wide.shape[0]):
        picked = jnp.where(lane_ids(TILE) == r, columns[rows, :], 0.0)
        wide[rows, :] = jnp.broadcast_to(jnp.sum(picked, axis=1, keepdims=True), (TILE, LANES))


def to_columns(source, columns):
    count, points = source.shape
    full = jnp.concatenate([source, jnp.zeros((LANES - count, points), jnp.float32)], axis=0)
    columns[...] = full.T


def stacked(tables, height):
    rest = height - sum(table.shape[0] for table in tables)
    if rest:
        tables = tables + [jnp.zeros((rest, LANES), jnp.float32)]
    return jnp.concatenate(tables, axis=0)


def exact_dot(marked, table, dim):
    return lax.dot_general(
        marked,
        table,
        (((dim,), (0,)), ((), ())),
        precision=lax.Precision.HIGHEST,
        preferred_element_type=jnp.float32,
    )


def row_first_kernel(
    unroll, picks_hbm, cost_hbm, source_hbm, target_hbm,
    plan, out, lows_out, source_mass, target_mass, marks,
    picks, cost, sems, wide, lows, totals,
):
    count, width, points, others = cost.shape

    def copy(r):
        return pltpu.make_async_copy(cost_hbm.at[r], cost.at[r], sems.at[r])

    pick = pltpu.make_async_copy(picks_hbm, picks, sems.at[count + 2])
    pick.start()
    for r in range(count):
        copy(r).start()
    copies = [
        pltpu.make_async_copy(source_hbm, source_mass, sems.at[count]),
        pltpu.make_async_copy(target_hbm, target_mass, sems.at[count + 1]),
    ]
    for other in copies:
        other.start()

    pick.wait()
    split, targets = others // LANES, target_mass.shape[0]
    for r in range(count):
        for n in range(width * split):
            k, h = divmod(n, split)
            spot = h * targets + picks[k, r]
            marks[r, n : n + 1, :] = jnp.where(lane_ids(1, marks.shape[2]) == spot, 1.0, 0.0)

    def body(r, carry):
        copy(r).wait()
        spots = [(k, pl.ds(lane, LANES)) for k in range(width) for lane in range(0, others, LANES)]
        for rows in tiles_of(points):
            low = None
            for n, (k, part) in enumerate(spots):
                value = cost[r, k, rows, part].astype(jnp.float32)
                plan[r, n, rows, :] = value
                low = value if low is None else jnp.minimum(low, value)
            wide[rows, :] = jnp.broadcast_to(jnp.min(low, axis=1, keepdims=True), (TILE, LANES))
        for rows in tiles_of(points):
            low = wide[rows, :]
            total = jnp.zeros((TILE, LANES), jnp.float32)
            for n in range(len(spots)):
                term = jnp.exp2((low - plan[r, n, rows, :]) * SCALE)
                plan[r, n, rows, :] = term
                total += term
            put_column(lows, rows, low, r)
            put_column(totals, rows, jnp.sum(total, axis=1, keepdims=True), r)
        return carry

    lax.fori_loop(0, count, body, 0, unroll=unroll)
    lows_out[...] = lows[...].T[:count] * SCALE
    out[...] = log2(totals[...].T[:count]) - lows_out[...]
    for other in copies:
        other.wait()


def col_first_kernel(
    unroll, picks_hbm, cost_hbm, plan_in, source, lows, marks,
    out, plan, peaks, base,
    picks, sems, cost, found, wide, columns,
):
    base[...] = source[...] - lows[...]
    peaks[...] = jnp.zeros(peaks.shape, jnp.float32)
    to_columns(jnp.exp2(base[...]), columns)
    count, parts, points, _ = plan.shape
    targets, others = out.shape
    split, height = others // LANES, marks.shape[2]
    tiles = tiles_of(points)

    def work(r, carry):
        spread_column(columns, wide, r)
        for n in range(parts):
            total = jnp.zeros((TILE, LANES), jnp.float32)
            for rows in tiles:
                total += plan_in[r, n, rows, :] * wide[rows, :]
            found[r, pl.ds(n, 1), :] = jnp.sum(total, axis=0, keepdims=True)
        return carry

    lax.fori_loop(0, count, work, 0, unroll=unroll)

    ample = jnp.min(found[...]) >= SMALLEST
    marked = marks[...].reshape(count * parts, height)

    def put_scores(sums, best):
        for h in range(split):
            total = sums[h * targets : (h + 1) * targets]
            named = total > 0.0
            score = best[h] + log2(jnp.where(named, total, 1.0))
            out[:, h * LANES : (h + 1) * LANES] = jnp.where(named, score, LOWEST)

    @pl.when(ample)
    def _():
        put_scores(exact_dot(marked, found[...].reshape(count * parts, LANES), 0), [0.0] * split)

    @pl.when(jnp.logical_not(ample))
    def _():
        copy = pltpu.make_async_copy(picks_hbm, picks, sems.at[0])
        copy.start()
        to_columns(source[...], columns)
        base[...] = jnp.zeros(base.shape, jnp.float32)

        def again(r, carry):
            block = pltpu.make_async_copy(cost_hbm.at[r], cost, sems.at[1])
            block.start()
            spread_column(columns, wide, r)
            block.wait()
            for n in range(parts):
                k, h = divmod(n, split)
                part = pl.ds(h * LANES, LANES)
                peak = None
                for rows in tiles:
                    value = wide[rows, :] - cost[k, rows, part].astype(jnp.float32) * SCALE
                    peak = value if peak is None else jnp.maximum(peak, value)
                peak = jnp.max(peak, axis=0, keepdims=True)
                total = jnp.zeros((TILE, LANES), jnp.float32)
                for rows in tiles:
                    value = wide[rows, :] - cost[k, rows, part].astype(jnp.float32) * SCALE
                    term = jnp.exp2(value - peak)
                    plan[r, n, rows, :] = term
                    total += term
                peaks[r, pl.ds(n, 1), :] = peak
                found[r, pl.ds(n, 1), :] = jnp.sum(total, axis=0, keepdims=True)
            return carry

        lax.fori_loop(0, count, again, 0)

        found[...] = peaks[...] + log2(found[...])
        copy.wait()

        own = lax.broadcasted_iota(jnp.int32, (targets, LANES), 0)

        def settle(r, best):
            best = list(best)
            for n in range(parts):
                k, h = divmod(n, split)
                mine = jnp.where(own == picks[k, r], found[r, pl.ds(n, 1), :], LOWEST)
                best[h] = jnp.maximum(best[h], mine)
            return tuple(best)

        lowest = jnp.full((targets, LANES), LOWEST, jnp.float32)
        best = lax.fori_loop(0, count, settle, (lowest,) * split)
        mine = exact_dot(marked, stacked(list(best), height), 1)
        terms = jnp.exp2(found[...].reshape(count * parts, LANES) - mine)
        put_scores(exact_dot(marked, terms, 0), best)


def row_next_kernel(unroll, plan, peaks, marks, target, base, out, lifts, totals):
    count, parts, points, _ = plan.shape
    height = marks.shape[2]
    marked = marks[...].reshape(count * parts, height)
    tables = [target[:, lane : lane + LANES] for lane in range(0, target.shape[1], LANES)]
    mine = exact_dot(marked, stacked(tables, height), 1)
    lifts[...] = jnp.exp2(mine.reshape(lifts.shape) + peaks[...])

    def body(r, carry):
        for rows in tiles_of(points):
            total = jnp.zeros((TILE, LANES), jnp.float32)
            for n in range(parts):
                total += plan[r, n, rows, :] * lifts[r, pl.ds(n, 1), :]
            put_column(totals, rows, jnp.sum(total, axis=1, keepdims=True), r)
        return carry

    lax.fori_loop(0, count, body, 0, unroll=unroll)
    out[...] = totals[...].T[:count] * jnp.exp2(base[...])


def col_next_kernel(
    unroll, plan, lifts, marks, source, change, base, out, source_hbm, result, sem, found, wide, columns
):
    count, parts, points, _ = plan.shape
    height = marks.shape[2]
    to_columns(jnp.exp2(change[...] + base[...]), columns)
    result[...] = (source[...] + change[...]) * (1.0 / SCALE)
    copy = pltpu.make_async_copy(result, source_hbm, sem)
    copy.start()

    def body(r, carry):
        spread_column(columns, wide, r)
        for n in range(parts):
            total = jnp.zeros((TILE, LANES), jnp.float32)
            for rows in tiles_of(points):
                total += plan[r, n, rows, :] * wide[rows, :]
            found[r, pl.ds(n, 1), :] = jnp.sum(total, axis=0, keepdims=True) * lifts[r, pl.ds(n, 1), :]
        return carry

    lax.fori_loop(0, count, body, 0, unroll=unroll)
    sums = exact_dot(
        marks[...].reshape(count * parts, height), found[...].reshape(count * parts, LANES), 0
    )
    targets, others = out.shape
    for h in range(others // LANES):
        out[:, h * LANES : (h + 1) * LANES] = sums[h * targets : (h + 1) * targets]
    copy.wait()


VMEM = pl.BlockSpec(memory_space=pltpu.VMEM)
HBM = pl.BlockSpec(memory_space=pltpu.HBM)
COPY = pltpu.SemaphoreType.DMA


def call(name, kernel, outs, specs, scratch, megabytes, args, aliases=()):
    return pl.pallas_call(
        kernel,
        out_shape=outs,
        in_specs=specs,
        out_specs=[HBM if isinstance(out, jax.ShapeDtypeStruct) else VMEM for out in outs],
        scratch_shapes=scratch,
        compiler_params=pltpu.CompilerParams(vmem_limit_bytes=megabytes << 20),
        name=name,
        input_output_aliases=dict(aliases),
    )(*args)


def in_hbm(value):
    return pltpu.with_memory_space_constraint(value, pltpu.HBM)


def per_device(rows, cols, block_cost, candidates, source_logmass, target_logmass):
    count, width, points, others = block_cost.shape
    targets = target_logmass.shape[0]
    parts = width * others // LANES
    assert count <= LANES and points % TILE == 0 and others % LANES == 0 and ITERS == 2
    height = -(-targets * (others // LANES) // LANES) * LANES
    f32 = jnp.float32
    by_source = pltpu.VMEM((count, points), f32)
    by_target = pltpu.VMEM((targets, others), f32)
    blocks = pltpu.VMEM((count, parts, points, LANES), f32)
    strips = pltpu.VMEM((count, parts, LANES), f32)
    marks = pltpu.VMEM((count, parts, height), f32)
    tall = pltpu.VMEM((points, LANES), f32)
    everyone = ("row", "col")
    n = rows * cols

    picks = candidates.T
    plan, scores, lows, source_mass, target_mass, marks = call(
        "row_first",
        functools.partial(row_first_kernel, UNROLL),
        [blocks, by_source, by_source, by_source, by_target, marks],
        [HBM, HBM, HBM, HBM],
        [pltpu.SMEM(picks.shape, picks.dtype), pltpu.VMEM(block_cost.shape, block_cost.dtype), COPY((count + 3,)), tall, tall, tall],
        GRANT,
        [in_hbm(picks), in_hbm(block_cost), in_hbm(source_logmass), in_hbm(target_logmass)],
    )
    source = source_mass * LOG2E - all_lse2(scores, "col", cols, (2,))
    scores, plan, peaks, base = call(
        "col_first",
        functools.partial(col_first_kernel, UNROLL),
        [by_target, blocks, strips, by_source],
        [HBM, HBM, VMEM, VMEM, VMEM, VMEM],
        [pltpu.SMEM(picks.shape, picks.dtype), COPY((2,)), pltpu.VMEM(block_cost.shape[1:], block_cost.dtype)]
        + [strips, tall, tall],
        GRANT,
        [in_hbm(picks), in_hbm(block_cost), plan, source, lows, marks],
        [(2, 1)],
    )
    target = target_mass * LOG2E - all_lse2(scores, everyone, n, (1, 2))
    sums, lifts = call(
        "row_next",
        functools.partial(row_next_kernel, UNROLL),
        [by_source, strips],
        [VMEM] * 5,
        [tall],
        8,
        [plan, peaks, marks, target, base],
    )
    change = source_mass * LOG2E - log2(all_sum(sums, "col", cols, (2,)))
    sums, source = call(
        "col_next",
        functools.partial(col_next_kernel, UNROLL),
        [by_target, jax.ShapeDtypeStruct((count, points), f32)],
        [VMEM] * 6,
        [by_source, COPY, strips, tall, tall],
        8,
        [plan, lifts, marks, source, change, base],
    )
    target = target + (target_mass * LOG2E - log2(all_sum(sums, everyone, n, (1, 2))))
    return (source, target * (1.0 / SCALE))


def solution(mesh):
    return jax.shard_map(
        functools.partial(per_device, mesh.shape["row"], mesh.shape["col"]),
        mesh=mesh,
        in_specs=(P("row", "col", None, None), P("row", "col"), P("row", None), P()),
        out_specs=(P("row", None), P()),
        check_vma=False,
    )
```

```python
import functools
import math

import jax
import jax.numpy as jnp
from jax import lax
from jax.experimental import pallas as pl
from jax.experimental.pallas import tpu as pltpu
from jax.sharding import PartitionSpec as P

ITERS = 2
EPS = 0.05
LOWEST = -1e30
SMALLEST = 2.0**-20
LOG2E = math.log2(math.e)
SCALE = LOG2E / EPS
LANES = 128
TILE = 16
UNROLL = 8
GRANT = 14


def log2(x):
    return jnp.log(x) * LOG2E


def add_exp2(a, b):
    high = jnp.maximum(a, b)
    return high + log2(1.0 + jnp.exp2(jnp.minimum(a, b) - high))


def bit_groups(size, sizes):
    bits = [1 << b for b in range(size.bit_length() - 1)]
    assert 1 << len(bits) == size
    groups = []
    while bits:
        take = sizes.pop(0) if sizes else 2
        groups.append(bits[:take])
        bits = bits[take:]
    return groups


def exchange(value, axes, size, bits):
    got = [value]
    offsets = [0]
    for bit in bits:
        offsets += [o | bit for o in offsets]
    for offset in offsets[1:]:
        got.append(lax.ppermute(value, axes, [(i, i ^ offset) for i in range(size)]))
    return got


def all_sum(value, axes, size, sizes):
    for bits in bit_groups(size, list(sizes)):
        value = functools.reduce(jnp.add, exchange(value, axes, size, bits))
    return value


def all_lse2(value, axes, size, sizes):
    for bits in bit_groups(size, list(sizes)):
        got = exchange(value, axes, size, bits)
        high = functools.reduce(jnp.maximum, got)
        value = high + log2(functools.reduce(jnp.add, [jnp.exp2(g - high) for g in got]))
    return value


def tiles_of(points):
    return [pl.ds(start, TILE) for start in range(0, points, TILE)]


def lane_ids(rows, width=LANES):
    return lax.broadcasted_iota(jnp.int32, (rows, width), 1)


def put_column(columns, rows, column, r):
    columns[rows, :] = jnp.where(lane_ids(TILE) == r, column, columns[rows, :])


def spread_column(columns, wide, r):
    for rows in tiles_of(wide.shape[0]):
        picked = jnp.where(lane_ids(TILE) == r, columns[rows, :], 0.0)
        wide[rows, :] = jnp.broadcast_to(jnp.sum(picked, axis=1, keepdims=True), (TILE, LANES))


def to_columns(source, columns):
    count, points = source.shape
    full = jnp.concatenate([source, jnp.zeros((LANES - count, points), jnp.float32)], axis=0)
    columns[...] = full.T


def stacked(tables, height):
    rest = height - sum(table.shape[0] for table in tables)
    if rest:
        tables = tables + [jnp.zeros((rest, LANES), jnp.float32)]
    return jnp.concatenate(tables, axis=0)


def exact_dot(marked, table, dim):
    return lax.dot_general(
        marked,
        table,
        (((dim,), (0,)), ((), ())),
        precision=lax.Precision.HIGHEST,
        preferred_element_type=jnp.float32,
    )


def row_first_kernel(
    unroll, picks_hbm, cost_hbm, source_hbm, target_hbm,
    plan, out, lows_out, source_mass, target_mass, marks,
    picks, cost, sems, wide, lows, totals,
):
    count, width, points, others = cost.shape

    def copy(r):
        return pltpu.make_async_copy(cost_hbm.at[r], cost.at[r], sems.at[r])

    pick = pltpu.make_async_copy(picks_hbm, picks, sems.at[count + 2])
    pick.start()
    for r in range(count):
        copy(r).start()
    copies = [
        pltpu.make_async_copy(source_hbm, source_mass, sems.at[count]),
        pltpu.make_async_copy(target_hbm, target_mass, sems.at[count + 1]),
    ]
    for other in copies:
        other.start()

    pick.wait()
    split, targets = others // LANES, target_mass.shape[0]
    for r in range(count):
        for n in range(width * split):
            k, h = divmod(n, split)
            spot = h * targets + picks[k, r]
            marks[r, n : n + 1, :] = jnp.where(lane_ids(1, marks.shape[2]) == spot, 1.0, 0.0)

    def body(r, carry):
        copy(r).wait()
        spots = [(k, pl.ds(lane, LANES)) for k in range(width) for lane in range(0, others, LANES)]
        for rows in tiles_of(points):
            low = None
            for n, (k, part) in enumerate(spots):
                value = cost[r, k, rows, part].astype(jnp.float32)
                plan[r, n, rows, :] = value
                low = value if low is None else jnp.minimum(low, value)
            wide[rows, :] = jnp.broadcast_to(jnp.min(low, axis=1, keepdims=True), (TILE, LANES))
        for rows in tiles_of(points):
            low = wide[rows, :]
            total = jnp.zeros((TILE, LANES), jnp.float32)
            for n in range(len(spots)):
                term = jnp.exp2((low - plan[r, n, rows, :]) * SCALE)
                plan[r, n, rows, :] = term
                total += term
            put_column(lows, rows, low, r)
            put_column(totals, rows, jnp.sum(total, axis=1, keepdims=True), r)
        return carry

    lax.fori_loop(0, count, body, 0, unroll=unroll)
    lows_out[...] = lows[...].T[:count] * SCALE
    out[...] = log2(totals[...].T[:count]) - lows_out[...]
    for other in copies:
        other.wait()


def col_first_kernel(
    unroll, picks_hbm, cost_hbm, plan_in, source, lows, marks,
    out, plan, peaks, base,
    picks, sems, cost, found, wide, columns,
):
    base[...] = source[...] - lows[...]
    peaks[...] = jnp.zeros(peaks.shape, jnp.float32)
    to_columns(jnp.exp2(base[...]), columns)
    count, parts, points, _ = plan.shape
    targets, others = out.shape
    split, height = others // LANES, marks.shape[2]
    tiles = tiles_of(points)

    def work(r, carry):
        spread_column(columns, wide, r)
        for n in range(parts):
            total = jnp.zeros((TILE, LANES), jnp.float32)
            for rows in tiles:
                total += plan_in[r, n, rows, :] * wide[rows, :]
            found[r, pl.ds(n, 1), :] = jnp.sum(total, axis=0, keepdims=True)
        return carry

    lax.fori_loop(0, count, work, 0, unroll=unroll)

    ample = jnp.min(found[...]) >= SMALLEST
    marked = marks[...].reshape(count * parts, height)

    def put_scores(sums, best):
        for h in range(split):
            total = sums[h * targets : (h + 1) * targets]
            named = total > 0.0
            score = best[h] + log2(jnp.where(named, total, 1.0))
            out[:, h * LANES : (h + 1) * LANES] = jnp.where(named, score, LOWEST)

    @pl.when(ample)
    def _():
        put_scores(exact_dot(marked, found[...].reshape(count * parts, LANES), 0), [0.0] * split)

    @pl.when(jnp.logical_not(ample))
    def _():
        copy = pltpu.make_async_copy(picks_hbm, picks, sems.at[0])
        copy.start()
        to_columns(source[...], columns)
        base[...] = jnp.zeros(base.shape, jnp.float32)

        def again(r, carry):
            block = pltpu.make_async_copy(cost_hbm.at[r], cost, sems.at[1])
            block.start()
            spread_column(columns, wide, r)
            block.wait()
            for n in range(parts):
                k, h = divmod(n, split)
                part = pl.ds(h * LANES, LANES)
                peak = None
                for rows in tiles:
                    value = wide[rows, :] - cost[k, rows, part].astype(jnp.float32) * SCALE
                    peak = value if peak is None else jnp.maximum(peak, value)
                peak = jnp.max(peak, axis=0, keepdims=True)
                total = jnp.zeros((TILE, LANES), jnp.float32)
                for rows in tiles:
                    value = wide[rows, :] - cost[k, rows, part].astype(jnp.float32) * SCALE
                    term = jnp.exp2(value - peak)
                    plan[r, n, rows, :] = term
                    total += term
                peaks[r, pl.ds(n, 1), :] = peak
                found[r, pl.ds(n, 1), :] = jnp.sum(total, axis=0, keepdims=True)
            return carry

        lax.fori_loop(0, count, again, 0)

        found[...] = peaks[...] + log2(found[...])
        copy.wait()

        own = lax.broadcasted_iota(jnp.int32, (targets, LANES), 0)

        def settle(r, best):
            best = list(best)
            for n in range(parts):
                k, h = divmod(n, split)
                mine = jnp.where(own == picks[k, r], found[r, pl.ds(n, 1), :], LOWEST)
                best[h] = jnp.maximum(best[h], mine)
            return tuple(best)

        lowest = jnp.full((targets, LANES), LOWEST, jnp.float32)
        best = lax.fori_loop(0, count, settle, (lowest,) * split)
        mine = exact_dot(marked, stacked(list(best), height), 1)
        terms = jnp.exp2(found[...].reshape(count * parts, LANES) - mine)
        put_scores(exact_dot(marked, terms, 0), best)


def row_next_kernel(unroll, plan, peaks, marks, target, base, out, lifts, totals):
    count, parts, points, _ = plan.shape
    height = marks.shape[2]
    marked = marks[...].reshape(count * parts, height)
    tables = [target[:, lane : lane + LANES] for lane in range(0, target.shape[1], LANES)]
    mine = exact_dot(marked, stacked(tables, height), 1)
    lifts[...] = jnp.exp2(mine.reshape(lifts.shape) + peaks[...])

    def body(r, carry):
        for rows in tiles_of(points):
            total = jnp.zeros((TILE, LANES), jnp.float32)
            for n in range(parts):
                total += plan[r, n, rows, :] * lifts[r, pl.ds(n, 1), :]
            put_column(totals, rows, jnp.sum(total, axis=1, keepdims=True), r)
        return carry

    lax.fori_loop(0, count, body, 0, unroll=unroll)
    out[...] = totals[...].T[:count] * jnp.exp2(base[...])


def col_next_kernel(
    unroll, plan, lifts, marks, source, change, base, out, source_hbm, result, sem, found, wide, columns
):
    count, parts, points, _ = plan.shape
    height = marks.shape[2]
    to_columns(jnp.exp2(change[...] + base[...]), columns)
    result[...] = (source[...] + change[...]) * (1.0 / SCALE)
    copy = pltpu.make_async_copy(result, source_hbm, sem)
    copy.start()

    def body(r, carry):
        spread_column(columns, wide, r)
        for n in range(parts):
            total = jnp.zeros((TILE, LANES), jnp.float32)
            for rows in tiles_of(points):
                total += plan[r, n, rows, :] * wide[rows, :]
            found[r, pl.ds(n, 1), :] = jnp.sum(total, axis=0, keepdims=True) * lifts[r, pl.ds(n, 1), :]
        return carry

    lax.fori_loop(0, count, body, 0, unroll=unroll)
    sums = exact_dot(
        marks[...].reshape(count * parts, height), found[...].reshape(count * parts, LANES), 0
    )
    targets, others = out.shape
    for h in range(others // LANES):
        out[:, h * LANES : (h + 1) * LANES] = sums[h * targets : (h + 1) * targets]
    copy.wait()


VMEM = pl.BlockSpec(memory_space=pltpu.VMEM)
HBM = pl.BlockSpec(memory_space=pltpu.HBM)
COPY = pltpu.SemaphoreType.DMA


def call(name, kernel, outs, specs, scratch, megabytes, args, aliases=()):
    return pl.pallas_call(
        kernel,
        out_shape=outs,
        in_specs=specs,
        out_specs=[HBM if isinstance(out, jax.ShapeDtypeStruct) else VMEM for out in outs],
        scratch_shapes=scratch,
        compiler_params=pltpu.CompilerParams(vmem_limit_bytes=megabytes << 20),
        name=name,
        input_output_aliases=dict(aliases),
    )(*args)


def in_hbm(value):
    return pltpu.with_memory_space_constraint(value, pltpu.HBM)


def per_device(rows, cols, block_cost, candidates, source_logmass, target_logmass):
    count, width, points, others = block_cost.shape
    targets = target_logmass.shape[0]
    parts = width * others // LANES
    assert count <= LANES and points % TILE == 0 and others % LANES == 0 and ITERS == 2
    height = -(-targets * (others // LANES) // LANES) * LANES
    f32 = jnp.float32
    by_source = pltpu.VMEM((count, points), f32)
    by_target = pltpu.VMEM((targets, others), f32)
    blocks = pltpu.VMEM((count, parts, points, LANES), f32)
    strips = pltpu.VMEM((count, parts, LANES), f32)
    marks = pltpu.VMEM((count, parts, height), f32)
    tall = pltpu.VMEM((points, LANES), f32)
    everyone = ("row", "col")
    n = rows * cols

    picks = candidates.T
    plan, scores, lows, source_mass, target_mass, marks = call(
        "row_first",
        functools.partial(row_first_kernel, UNROLL),
        [blocks, by_source, by_source, by_source, by_target, marks],
        [HBM, HBM, HBM, HBM],
        [pltpu.SMEM(picks.shape, picks.dtype), pltpu.VMEM(block_cost.shape, block_cost.dtype), COPY((count + 3,)), tall, tall, tall],
        GRANT,
        [in_hbm(picks), in_hbm(block_cost), in_hbm(source_logmass), in_hbm(target_logmass)],
    )
    source = source_mass * LOG2E - all_lse2(scores, "col", cols, (2,))
    scores, plan, peaks, base = call(
        "col_first",
        functools.partial(col_first_kernel, 16),
        [by_target, blocks, strips, by_source],
        [HBM, HBM, VMEM, VMEM, VMEM, VMEM],
        [pltpu.SMEM(picks.shape, picks.dtype), COPY((2,)), pltpu.VMEM(block_cost.shape[1:], block_cost.dtype)]
        + [strips, tall, tall],
        GRANT,
        [in_hbm(picks), in_hbm(block_cost), plan, source, lows, marks],
        [(2, 1)],
    )
    target = target_mass * LOG2E - all_lse2(scores, everyone, n, (1, 2))
    sums, lifts = call(
        "row_next",
        functools.partial(row_next_kernel, 16),
        [by_source, strips],
        [VMEM] * 5,
        [tall],
        8,
        [plan, peaks, marks, target, base],
    )
    change = source_mass * LOG2E - log2(all_sum(sums, "col", cols, (2,)))
    sums, source = call(
        "col_next",
        functools.partial(col_next_kernel, UNROLL),
        [by_target, jax.ShapeDtypeStruct((count, points), f32)],
        [VMEM] * 6,
        [by_source, COPY, strips, tall, tall],
        8,
        [plan, lifts, marks, source, change, base],
    )
    target = target + (target_mass * LOG2E - log2(all_sum(sums, everyone, n, (1, 2))))
    return (source, target * (1.0 / SCALE))


def solution(mesh):
    return jax.shard_map(
        functools.partial(per_device, mesh.shape["row"], mesh.shape["col"]),
        mesh=mesh,
        in_specs=(P("row", "col", None, None), P("row", "col"), P("row", None), P()),
        out_specs=(P("row", None), P()),
        check_vma=False,
    )
```
